128 devices in a mesh: section: 8 (over z, core), ctx: 16 (over y, x).
Axes of the slice: x: 4, y: 4, z: 4, core: 2. Of those that a mesh axis runs over, the one named last changes fastest.
Arguments:
- spins: int32 [8, 2048], replicated, may hold values from 0 to 1
- block_mask: int32 [16, 16], P('ctx'), may hold values from 0 to 1, as said below
- tok_embed: float32 [3, 1024], replicated, may hold values from -6 to 6
- pos_embed: bfloat16 [2048, 1024], P('ctx'), may hold values from -6 to 6
- norm1_gain: float32 [8, 1024], P('section'), may hold values from 0.1 to 1.9
- w_qkv: bfloat16 [8, 1024, 3072], P('section')
- w_out: bfloat16 [8, 1024, 1024], P('section'), may hold values from -0.1875 to 0.1875
- norm2_gain: float32 [8, 1024], P('section'), may hold values from 0.1 to 1.9
- w_up: bfloat16 [8, 1024, 2048], P('section'), may hold values from -0.1875 to 0.1875
- w_down: bfloat16 [8, 2048, 1024], P('section'), may hold values from -0.125 to 0.125
- w_head: float32 [1024], replicated, may hold values from -0.1875 to 0.1875
Outputs:
- log_amplitude: float32 [8, 2048], P('section', 'ctx')
The draws below stay inside these ranges and needn't reach their ends.
Inputs may be any that keep to these rules, and one draw needn't show every extreme that they name: block_mask[q, k] is 1 where k = q, and where k = q - 1; where q - k = 2 ** j with 1 <= j < 3 it is 0 or 1; it is 0 everywhere else.
All inputs are finite; a program needn't handle non-finite values.
Results may differ from the reference program's by a relative error of at most 0.012.
Values may be sent and summed in bfloat16 or wider, within the bound.
No kernel may reach another device: no remote copies, remote signals or barrier semaphores. Data moves between devices by JAX's collectives and lax.ppermute only.
A program may use at most 64 MiB of HBM per device.

```python
import math
import jax
import jax.numpy as jnp
from jax import lax

D = 1024
HEADS = 16
FF = 2048
BLOCK = 128
NDIL = 3
LAYERS = 8
SAMPLES = 8
L = 2048
NBLK = 16


def draw_block_mask(key, part):
    query_index = jnp.arange(NBLK, dtype=jnp.int32)[:, None]
    key_index = jnp.arange(NBLK, dtype=jnp.int32)[None, :]
    distance = query_index - key_index
    coins = jax.random.randint(key, (NBLK, NBLK), 0, 2)
    dilated = jnp.zeros((NBLK, NBLK), jnp.bool_)
    for level_index in range(1, NDIL):
        dilated = dilated | (distance == 2 ** level_index)
    local = (distance == 0) | (distance == 1)
    return jnp.where(local, 1, jnp.where(dilated, coins, 0)).astype(jnp.int32)


def draw_w_qkv(key, part):
    base = jnp.clip(jax.random.normal(key, (LAYERS, D, 3 * D), jnp.float32), -6.0, 6.0) * D ** (-0.5)
    return base.astype(jnp.bfloat16)


def touch_ends(result, stream_key, least, high):
    dims = result.shape
    index_at = [jax.random.randint(jax.random.fold_in(stream_key, axis), (), 0, dims[axis]) for axis in range(len(dims))]
    result = result.at[tuple(index_at)].set(least)
    longest = dims.index(max(dims))
    index_at[longest] = (index_at[longest] + 1) % dims[longest]
    return result.at[tuple(index_at)].set(high)


def steps_of(stream_key, dims, pieces, least, high):
    loudness = 1.0
    for position, parts in pieces:
        heights = jax.random.uniform(jax.random.fold_in(jax.random.fold_in(stream_key, 6), position), (parts,), jnp.float32, least / len(pieces), high / len(pieces))
        loudness = loudness * jnp.repeat(jnp.exp(heights), dims[position] // parts).reshape((-1,) + (1,) * (len(dims) - 1 - position))
    return loudness


def noise(rng, shape, spread, most, shards=(), kind=jnp.bfloat16):
    result = jax.random.normal(rng, shape, jnp.float32) * spread
    if len(shards) > 0:
        result = steps_of(rng, shape, shards, -0.22, 0.18) * result
    return jnp.clip(result, min=-most, max=most).astype(kind)


def setup_inputs(seed: int = 0) -> dict:
    arg_keys = jax.random.split(jax.random.key(seed), 12)
    spins = touch_ends(jax.random.randint(arg_keys[0], (SAMPLES, L), 0, 2), jax.random.fold_in(arg_keys[0], 1), 0, 1).astype(jnp.int32)
    block_mask = draw_block_mask(jax.random.fold_in(arg_keys[11], 71), 0)
    tok_embed = noise(arg_keys[2], (3, D), 1.0, 6.0, (), jnp.float32)
    pos_embed = noise(arg_keys[3], (L, D), 1.0, 6.0, ((0, 16),))
    norm1_gain = jnp.clip(1.0 + 0.18 * jax.random.normal(arg_keys[4], (LAYERS, D), jnp.float32), 0.1, 1.9)
    w_qkv = draw_w_qkv(jax.random.fold_in(arg_keys[11], 71), 0)
    w_out = noise(arg_keys[6], (LAYERS, D, D), D ** -0.5, 0.1875, ((0, 8),))
    norm2_gain = jnp.clip(1.0 + 0.18 * jax.random.normal(arg_keys[7], (LAYERS, D), jnp.float32), 0.1, 1.9)
    w_up = noise(arg_keys[8], (LAYERS, D, FF), D ** -0.5, 0.1875, ((0, 8),))
    w_down = noise(arg_keys[9], (LAYERS, FF, D), FF ** -0.5, 0.125, ((0, 8),))
    w_head = noise(arg_keys[10], (D,), D ** -0.5, 0.1875, (), jnp.float32)
    return dict(spins=spins, block_mask=block_mask, tok_embed=tok_embed, pos_embed=pos_embed, norm1_gain=norm1_gain, w_qkv=w_qkv, w_out=w_out, norm2_gain=norm2_gain, w_up=w_up, w_down=w_down, w_head=w_head)


def rms_normed(vector):
    return vector * lax.rsqrt(lax.optimization_barrier(jnp.mean(vector * vector, axis=-1, keepdims=True)) + 1e-05)

def attend(queries, key_rows, value_rows, block_mask):
    samples, length, head_count, head_dim = queries.shape
    block_count = length // BLOCK
    window = 2 ** (NDIL - 1) + 1
    padding = (window - 1) * BLOCK
    keys_padded = jnp.pad(key_rows, ((0, 0), (padding, 0), (0, 0), (0, 0)))
    values_padded = jnp.pad(value_rows, ((0, 0), (padding, 0), (0, 0), (0, 0)))
    key_slot = jnp.arange(window * BLOCK, dtype=jnp.int32)
    query_pos = jnp.arange(BLOCK, dtype=jnp.int32)

    def one_block(block_index):
        query_block = lax.dynamic_slice_in_dim(queries, block_index * BLOCK, BLOCK, 1).astype(jnp.float32)
        key_block = lax.dynamic_slice_in_dim(keys_padded, block_index * BLOCK, window * BLOCK, 1).astype(jnp.float32)
        value_block = lax.dynamic_slice_in_dim(values_padded, block_index * BLOCK, window * BLOCK, 1).astype(jnp.float32)
        scores = jnp.einsum('sqhd,skhd->shqk', query_block, key_block) / math.sqrt(head_dim)
        key_block_index = block_index - (window - 1) + key_slot // BLOCK
        key_pos = key_slot % BLOCK
        mask_row = lax.dynamic_index_in_dim(block_mask, block_index, 0, keepdims=False)
        picked = mask_row[jnp.clip(key_block_index, 0, block_count - 1)]
        earlier = (key_block_index >= 0) & (key_block_index < block_index) & (picked == 1)
        same_block = (key_block_index == block_index)[None, :] & (key_pos[None, :] <= query_pos[:, None])
        allowed = same_block | earlier[None, :]
        scores = jnp.where(allowed[None, None], scores, -jnp.inf)
        probs = jax.nn.softmax(scores, axis=-1).astype(jnp.bfloat16)
        mixed = jnp.einsum('shqk,skhd->sqhd', probs.astype(jnp.float32), value_block)
        return mixed.astype(jnp.bfloat16)
    blocks = lax.map(one_block, jnp.arange(block_count, dtype=jnp.int32))
    return jnp.transpose(blocks, (1, 0, 2, 3, 4)).reshape(samples, length, head_count * head_dim)

def reference(spins, block_mask, tok_embed, pos_embed, norm1_gain, w_qkv, w_out, norm2_gain, w_up, w_down, w_head):
    samples, length = spins.shape
    head_dim = D // HEADS
    previous = jnp.concatenate([jnp.full((samples, 1), 2, jnp.int32), spins[:, :-1]], axis=1)[..., None]
    embedded = jnp.where(previous == 0, tok_embed[0], jnp.where(previous == 1, tok_embed[1], tok_embed[2]))
    state = (embedded + pos_embed.astype(jnp.float32)[None]).astype(jnp.bfloat16)
    for layer_index in range(LAYERS):
        normed_rows = (rms_normed(state.astype(jnp.float32)) * norm1_gain[layer_index]).astype(jnp.bfloat16)
        projected = jnp.dot(normed_rows.reshape(-1, D), w_qkv[layer_index], preferred_element_type=jnp.float32)
        queries = projected[:, :D].astype(jnp.bfloat16).reshape(samples, length, HEADS, head_dim)
        key_rows = projected[:, D:2 * D].astype(jnp.bfloat16).reshape(samples, length, HEADS, head_dim)
        value_rows = projected[:, 2 * D:].astype(jnp.bfloat16).reshape(samples, length, HEADS, head_dim)
        attended = attend(queries, key_rows, value_rows, block_mask)
        hidden = state.astype(jnp.float32) + jnp.dot(attended.reshape(-1, D), w_out[layer_index], preferred_element_type=jnp.float32).reshape(samples, length, D)
        lifted = (rms_normed(hidden) * norm2_gain[layer_index]).astype(jnp.bfloat16)
        activated = jax.nn.gelu(jnp.dot(lifted.reshape(-1, D), w_up[layer_index], preferred_element_type=jnp.float32)).astype(jnp.bfloat16)
        state = (hidden + jnp.dot(activated, w_down[layer_index], preferred_element_type=jnp.float32).reshape(samples, length, D)).astype(jnp.bfloat16)
    final_rows = rms_normed(state.astype(jnp.float32))
    logits = jnp.dot(final_rows.reshape(-1, D), w_head, precision=lax.Precision.HIGHEST).reshape(samples, length)
    per_site_terms = math.log(2.0) - jax.nn.softplus((1.0 - 2.0 * spins.astype(jnp.float32)) * logits)
    return 0.5 * jnp.cumsum(per_site_terms, axis=1)
```

```python
import functools
import math

import jax
import jax.numpy as jnp
from jax import lax
from jax.experimental import pallas as pl
from jax.experimental.pallas import tpu as pltpu
from jax.sharding import PartitionSpec as P

F32, BF = jnp.float32, jnp.bfloat16
R = 128
H = 8
D, FF = 1024, 2048
PAIRS = 8
STAGES, CTX, MICRO = 8, 16, 8
TICKS = MICRO + 2 * (STAGES - 1)
NEG = -1e30
AX = ("section", "ctx")


def dev(s, c):
    return s * CTX + c


def rms_scale(v):
    return lax.rsqrt(jnp.mean(v * v, axis=-1, keepdims=True) + 1e-05)


def column_of(row):
    i = lax.broadcasted_iota(jnp.int32, (R, R), 0)
    j = lax.broadcasted_iota(jnp.int32, (R, R), 1)
    return jnp.sum(jnp.where(i == j, row, 0.0), axis=1, keepdims=True)


def layer_kernel(*refs, k, has_e, has_o, last_possible):
    it = iter(refs)
    info = next(it)
    e_ref = next(it) if has_e else None
    o_ref, ca_ref, cb_ref = (next(it), next(it), next(it)) if has_o else (None, None, None)
    kv2, kv4, wqkv, wout, wup, wdown, g1, g2, tok, whead, prev, own, run_in = [next(it) for _ in range(13)]
    out_ref, kvo, msg = next(it), next(it), next(it)
    x_s, h_s, kvc, q_s, att_s, hid_s, act_s = [next(it) for _ in range(7)]
    stage, odd = info[0], info[1]
    m = k - 2 * stage
    b = 2 * m + odd

    @pl.when((m == -1) | (m == -2))
    def _():
        kvo[...] = jnp.zeros_like(kvo)

    @pl.when((m >= 0) & (m < MICRO))
    def _():
        if has_e:
            @pl.when(stage == 0)
            def _():
                def embed(block, pos):
                    t = column_of(prev[pl.ds(jnp.maximum(block, 0), 1), :])
                    rows = jnp.where(t == 0.0, tok[0:1, :], jnp.where(t == 1.0, tok[1:2, :], tok[2:3, :]))
                    return (rows + pos.astype(F32)).astype(BF)

                x_s[0:R, :] = embed(b, e_ref[0:R, :])
                x_s[R:, :] = embed(b - 1, e_ref[R + H:2 * R + H, :])
                h_s[...] = e_ref[R:R + H, :]
        if has_o:
            @pl.when(stage > 0)
            def _():
                x_s[0:R, :] = o_ref[0:R, :]
                h_s[...] = o_ref[R:R + H, :]

                @pl.when(odd == 0)
                def _():
                    x_s[R:, :] = ca_ref[0:R, :]

                @pl.when(odd == 1)
                def _():
                    x_s[R:, :] = cb_ref[0:R, :]

        xf = x_s[...].astype(F32)
        a = (xf * rms_scale(xf) * g1[...]).astype(BF)
        q_s[...] = (jnp.dot(a[0:R, :], wqkv[:, :D], preferred_element_type=F32) * 0.125).astype(BF)
        for j in range(2):
            p = jnp.dot(a, wqkv[:, (j + 1) * D:(j + 2) * D], preferred_element_type=F32).astype(BF)
            kvo[:, j * D:(j + 1) * D] = p[:R]
            kvc[:, j * D:(j + 1) * D] = p[R:]

        lane = lax.broadcasted_iota(jnp.int32, (R, 128), 1)
        row = lax.broadcasted_iota(jnp.int32, (R, 128), 0)
        causal = jnp.where(lane <= row, 0.0, NEG)
        causal2 = jnp.concatenate([causal, causal], axis=0)
        flags = h_s[0:1, 0:384].astype(F32)
        f1, f2, f4 = [jnp.where(flags[:, i * 128:(i + 1) * 128] > 0.5, 0.0, NEG) for i in range(3)]
        ones = jnp.ones((2 * R, 128), BF)
        low = lane < 64
        nt = (((1,), (1,)), ((), ()))
        for h in range(PAIRS):
            o, v = slice(h * 128, h * 128 + 128), slice(D + h * 128, D + h * 128 + 128)
            q = q_s[:, o]
            zero = jnp.zeros_like(q)
            q2 = jnp.concatenate([jnp.where(low, q, zero), jnp.where(low, zero, q)], axis=0)
            ka = jnp.concatenate([kvo[:, o], kvc[:, o]], axis=0)
            kb = jnp.concatenate([kv2[:, o], kv4[:, o]], axis=0)
            sa = lax.dot_general(q2, ka, nt, preferred_element_type=F32)
            sb = lax.dot_general(q2, kb, nt, preferred_element_type=F32)
            s0 = sa[:, :128] + causal2
            s1 = sa[:, 128:] + f1
            s2 = sb[:, :128] + f2
            s4 = sb[:, 128:] + f4
            top = jnp.max(jnp.maximum(jnp.maximum(s0, s1), jnp.maximum(s2, s4)), axis=-1, keepdims=True)
            pa = jnp.concatenate([jnp.exp(s0 - top).astype(BF), jnp.exp(s1 - top).astype(BF)], axis=1)
            pb = jnp.concatenate([jnp.exp(s2 - top).astype(BF), jnp.exp(s4 - top).astype(BF)], axis=1)
            va = jnp.concatenate([jnp.concatenate([kvo[:, v], kvc[:, v]], axis=0), ones], axis=1)
            vb = jnp.concatenate([jnp.concatenate([kv2[:, v], kv4[:, v]], axis=0), ones], axis=1)
            r = jnp.dot(pa, va, preferred_element_type=F32) + jnp.dot(pb, vb, preferred_element_type=F32)
            num = jnp.where(low, r[:R, :128], r[R:, :128])
            den = jnp.where(low, r[:R, 128:], r[R:, 128:])
            att_s[:, o] = (num / den).astype(BF)

        hid_s[...] = x_s[0:R, :].astype(F32) + jnp.dot(att_s[...], wout[...], preferred_element_type=F32)
        hid = hid_s[...]
        lifted = (hid * rms_scale(hid) * g2[...]).astype(BF)
        for j in range(2):
            up = jnp.dot(lifted, wup[:, j * D:(j + 1) * D], preferred_element_type=F32)
            act_s[:, j * D:(j + 1) * D] = jax.nn.gelu(up).astype(BF)
        out = (hid_s[...] + jnp.dot(act_s[...], wdown[...], preferred_element_type=F32)).astype(BF)
        out_ref[0:R, :] = out
        out_ref[R:, :] = h_s[...]
        if last_possible:
            @pl.when(stage == STAGES - 1)
            def _():
                y = out_ref[0:R, :].astype(F32)
                logits = jnp.sum(y * rms_scale(y) * whead[...], axis=-1, keepdims=True)
                spin = column_of(own[pl.ds(b, 1), :])
                terms = math.log(2.0) - jax.nn.softplus((1.0 - 2.0 * spin) * logits)
                i = lax.broadcasted_iota(jnp.int32, (R, R), 0)
                j = lax.broadcasted_iota(jnp.int32, (R, R), 1)
                cum = jnp.sum(jnp.where(i <= j, terms, 0.0), axis=0, keepdims=True)
                tot = jnp.sum(jnp.broadcast_to(terms, (R, R)), axis=0, keepdims=True)
                run = run_in[1:2, :]
                msg[...] = jnp.concatenate([cum + run, tot + run, jnp.zeros((6, 128), F32)], axis=0)


def layer_call(k, info, e, o, ca, cb, rest, run):
    has_e, has_o = e is not None, o is not None
    vm = pl.BlockSpec(memory_space=pltpu.VMEM)
    args = ([e] if has_e else []) + ([o, ca, cb] if has_o else []) + list(rest) + [run]
    return pl.pallas_call(
        functools.partial(layer_kernel, k=k, has_e=has_e, has_o=has_o, last_possible=k >= 2 * (STAGES - 1)),
        out_shape=(
            jax.ShapeDtypeStruct((R + H, D), BF),
            jax.ShapeDtypeStruct((R, 2 * D), BF),
            jax.ShapeDtypeStruct((8, 128), F32),
        ),
        in_specs=[pl.BlockSpec(memory_space=pltpu.SMEM)] + [vm] * len(args),
        out_specs=(vm, vm, vm),
        scratch_shapes=[
            pltpu.VMEM((2 * R, D), BF),
            pltpu.VMEM((H, D), BF),
            pltpu.VMEM((R, 2 * D), BF),
            pltpu.VMEM((R, D), BF),
            pltpu.VMEM((R, D), BF),
            pltpu.VMEM((R, D), F32),
            pltpu.VMEM((R, FF), BF),
        ],
        compiler_params=pltpu.CompilerParams(vmem_limit_bytes=20 << 20),
        cost_estimate=pl.CostEstimate(flops=4 * 10**9, bytes_accessed=10**6, transcendentals=10**6),
        name=f"layer{k}",
    )(info, *args)


def body(spins, block_mask, tok_embed, pos_embed, norm1_gain, w_qkv, w_out, norm2_gain, w_up, w_down, w_head):
    stage = lax.axis_index("section")
    ctx = lax.axis_index("ctx")
    info = jnp.stack([stage, ctx % 2]).astype(jnp.int32)
    sample = ctx // 2
    mine = lax.dynamic_slice_in_dim(spins, sample, 1, 0)
    own = mine.astype(F32).reshape(CTX, R)
    prev = jnp.concatenate([jnp.full((1, 1), 2, jnp.int32), mine[:, :-1]], axis=1).astype(F32).reshape(CTX, R)

    def flag(distance):
        hit = (jnp.arange(CTX) == ctx - distance) & (block_mask[0] == 1)
        return jnp.broadcast_to(jnp.any(hit), (128,))

    header = jnp.concatenate([flag(1), flag(2), flag(4), jnp.zeros((D - 384,), jnp.bool_)]).astype(BF)
    message = jnp.concatenate([pos_embed, jnp.broadcast_to(header[None], (H, D))], axis=0)

    def send(value, pairs):
        return lax.ppermute(value, AX, pairs)

    first_own = send(message, [(dev(s, p), dev(0, 2 * s + p)) for s in range(STAGES) for p in range(2)])
    first_copy = send(message[:R], [(dev(s, 0), dev(0, 2 * s + 1)) for s in range(STAGES)])
    behind = send(pos_embed, [(dev(s, c), dev(s, c + 1)) for s in range(STAGES) for c in range(CTX - 1)])
    double = jnp.concatenate([message, behind], axis=0)
    feeds = [jnp.concatenate([first_own, first_copy], axis=0)]
    for m in range(1, MICRO):
        feeds.append(send(double, [(dev(s, 2 * m + p), dev(0, 2 * s + p)) for s in range(STAGES) for p in range(2)]))

    rest = (w_qkv[0], w_out[0], w_up[0], w_down[0], norm1_gain, norm2_gain, tok_embed, w_head[None], prev, own)
    kv_blank = jnp.zeros((R, 2 * D), BF)
    kvs = {-1: kv_blank, -2: kv_blank}
    owns, copies = {}, {}
    run = jnp.zeros((8, 128), F32)
    result = jnp.zeros((1, 128), F32)
    for k in range(TICKS):
        e = feeds[k] if k < MICRO else None
        o = owns.get(k - 2)
        cb = copies.get(k - 2)
        ca = copies.get(k - 3, cb)
        out, kvs[k], msg = layer_call(k, info, e, o, ca, cb, (kvs[k - 1], kvs[k - 2]) + rest, run)
        live = [s for s in range(STAGES) if 0 <= k - 2 * s < MICRO]
        senders = [s for s in live if s < STAGES - 1]
        if senders:
            owns[k] = send(out, [(dev(s, c), dev(s + 1, c)) for s in senders for c in range(CTX)])
            copies[k] = send(out, [(dev(s, c), dev(s + 1, c ^ 1)) for s in senders for c in range(CTX)])
        if STAGES - 1 in live:
            m = k - 2 * (STAGES - 1)
            run = msg
            a = send(msg, [(dev(STAGES - 1, 2 * n + p), dev(n, 2 * m + p)) for n in range(STAGES) for p in range(2)])
            z = send(
                msg,
                [
                    (dev(STAGES - 1, 2 * n + p), dev(n, 2 * m + p + 1))
                    for n in range(STAGES)
                    for p in range(2)
                    if 2 * m + p + 1 < CTX
                ],
            )
            result = result + a[0:1] + z[1:2]
    return 0.5 * result


def solution(mesh):
    return jax.shard_map(
        body,
        mesh=mesh,
        in_specs=(
            P(),
            P("ctx", None),
            P(),
            P("ctx", None),
            P("section", None),
            P("section", None, None),
            P("section", None, None),
            P("section", None),
            P("section", None, None),
            P("section", None, None),
            P(),
        ),
        out_specs=P("section", "ctx"),
        check_vma=False,
    )
```

```python
import functools
import math

import jax
import jax.numpy as jnp
from jax import lax
from jax.experimental import pallas as pl
from jax.experimental.pallas import tpu as pltpu
from jax.sharding import PartitionSpec as P

F32, BF = jnp.float32, jnp.bfloat16
R = 128
H = 8
D, FF = 1024, 2048
PAIRS = 8
STAGES, CTX, MICRO = 8, 16, 8
TICKS = MICRO + 2 * (STAGES - 1)
NEG = -1e30
AX = ("section", "ctx")


def dev(s, c):
    return s * CTX + c


def rms_scale(v):
    return lax.rsqrt(jnp.mean(v * v, axis=-1, keepdims=True) + 1e-05)


def shifted_column(row, before, shift):
    i = lax.broadcasted_iota(jnp.int32, (R, R), 0)
    j = lax.broadcasted_iota(jnp.int32, (R, R), 1)
    if not shift:
        return jnp.sum(jnp.where(i == j, row, 0.0), axis=1, keepdims=True)
    both = jnp.where(i == j + 1, row, 0.0) + jnp.where((i == 0) & (j == R - 1), before, 0.0)
    return jnp.sum(both, axis=1, keepdims=True)


def spin_row(spins, sample, block):
    start = pl.multiple_of(jnp.maximum(block, 0) * R, R)
    rows = spins[:, pl.ds(start, R)].astype(F32)
    return jnp.sum(jnp.where(lax.broadcasted_iota(jnp.int32, rows.shape, 0) == sample, rows, 0.0), axis=0, keepdims=True)


def feed_kernel(mask, pos, behind, out):
    ctx = lax.axis_index("ctx")
    out[0:R, :] = pos[...]
    out[R + H:, :] = behind[...]
    columns = lax.broadcasted_iota(jnp.int32, (1, 128), 1)
    row = mask[...]
    flags = []
    for distance in (1, 2, 4):
        at = lax.broadcasted_iota(jnp.int32, (1, CTX), 1)
        hit = jnp.sum(jnp.where((at == ctx - distance) & (row == 1), 1.0, 0.0), axis=1, keepdims=True)
        flags.append(jnp.broadcast_to(hit, (H, 128)))
    flags.append(jnp.zeros((H, D - 384), F32))
    out[R:R + H, :] = jnp.concatenate(flags, axis=1).astype(BF)


def feed_call(mask, pos, behind):
    vm = pl.BlockSpec(memory_space=pltpu.VMEM)
    return pl.pallas_call(
        feed_kernel,
        out_shape=jax.ShapeDtypeStruct((2 * R + H, D), BF),
        in_specs=[vm] * 3,
        out_specs=vm,
        compiler_params=pltpu.CompilerParams(vmem_limit_bytes=4 << 20),
        name="feed",
    )(mask, pos, behind)


def layer_kernel(*refs, k):
    it = iter(refs)
    first = [next(it) for _ in range(2)] if k == 0 else None
    e_ref = next(it) if 0 < k < MICRO else None
    has_o = k >= 2
    o_ref, ca_ref, cb_ref = (next(it), next(it), next(it)) if has_o else (None, None, None)
    kv2 = next(it) if k >= 1 else None
    kv4 = next(it) if k >= 2 else None
    last_possible = k >= 2 * (STAGES - 1)
    wqkv, wout, wup, wdown, g1, g2, tok, whead, spins = [next(it) for _ in range(9)]
    run_in = next(it) if k > 2 * (STAGES - 1) else None
    out_ref, kvo = next(it), next(it)
    msg = next(it) if last_possible else None
    x_s, h_s, kvc, q_s, att_s, hid_s, act_s = [next(it) for _ in range(7)]
    stage, ctx = lax.axis_index("section"), lax.axis_index("ctx")
    sample, odd = ctx // 2, ctx % 2
    m = k - 2 * stage
    b = 2 * m + odd

    if k < 2 * (STAGES - 1):
        @pl.when((m == -1) | (m == -2))
        def _():
            kvo[...] = jnp.zeros_like(kvo)

    @pl.when((m >= 0) & (m < MICRO))
    def _():
        if k < MICRO:
            @pl.when(stage == 0)
            def _():
                def embed(block, pos):
                    before = jnp.where(block > 0, spin_row(spins, sample, block - 1), 2.0)
                    t = shifted_column(spin_row(spins, sample, block), before, True)
                    rows = jnp.where(t == 0.0, tok[0:1, :], jnp.where(t == 1.0, tok[1:2, :], tok[2:3, :]))
                    return (rows + pos.astype(F32)).astype(BF)

                if k == 0:
                    x_s[0:R, :] = embed(b, first[0][...])
                    x_s[R:, :] = embed(b - 1, first[1][...])
                    lanes = lax.broadcasted_iota(jnp.int32, (H, D), 1)
                    h_s[...] = jnp.where((lanes < 128) & (odd == 1), 1.0, 0.0).astype(BF)
                else:
                    x_s[0:R, :] = embed(b, e_ref[0:R, :])
                    x_s[R:, :] = embed(b - 1, e_ref[R + H:2 * R + H, :])
                    h_s[...] = e_ref[R:R + H, :]
        if has_o:
            @pl.when(stage > 0)
            def _():
                x_s[0:R, :] = o_ref[0:R, :]
                h_s[...] = o_ref[R:R + H, :]

                @pl.when(odd == 0)
                def _():
                    x_s[R:, :] = ca_ref[0:R, :]

                @pl.when(odd == 1)
                def _():
                    x_s[R:, :] = cb_ref[0:R, :]

        xf = x_s[...].astype(F32)
        a = (xf * rms_scale(xf) * g1[...]).astype(BF)
        q_s[...] = (jnp.dot(a[0:R, :], wqkv[:, :D], preferred_element_type=F32) * 0.125).astype(BF)
        for j in range(2):
            p = jnp.dot(a, wqkv[:, (j + 1) * D:(j + 2) * D], preferred_element_type=F32).astype(BF)
            kvo[:, j * D:(j + 1) * D] = p[:R]
            kvc[:, j * D:(j + 1) * D] = p[R:]

        lane = lax.broadcasted_iota(jnp.int32, (R, 128), 1)
        row = lax.broadcasted_iota(jnp.int32, (R, 128), 0)
        causal = jnp.where(lane <= row, 0.0, NEG)
        causal2 = jnp.concatenate([causal, causal], axis=0)
        flags = h_s[0:1, 0:384].astype(F32)
        f1, f2, f4 = [jnp.where(flags[:, i * 128:(i + 1) * 128] > 0.5, 0.0, NEG) for i in range(3)]
        ones = jnp.ones((2 * R, 128), BF)
        low = lane < 64
        nt = (((1,), (1,)), ((), ()))
        for h in range(PAIRS):
            o, v = slice(h * 128, h * 128 + 128), slice(D + h * 128, D + h * 128 + 128)
            q = q_s[:, o]
            zero = jnp.zeros_like(q)
            q2 = jnp.concatenate([jnp.where(low, q, zero), jnp.where(low, zero, q)], axis=0)
            ka = jnp.concatenate([kvo[:, o], kvc[:, o]], axis=0)
            blank = jnp.zeros((R, 128), BF)
            kb = jnp.concatenate([kv2[:, o] if kv2 is not None else blank, kv4[:, o] if kv4 is not None else blank], axis=0)
            sa = lax.dot_general(q2, ka, nt, preferred_element_type=F32)
            sb = lax.dot_general(q2, kb, nt, preferred_element_type=F32)
            s0 = sa[:, :128] + causal2
            s1 = sa[:, 128:] + f1
            s2 = sb[:, :128] + f2
            s4 = sb[:, 128:] + f4
            top = jnp.max(jnp.maximum(jnp.maximum(s0, s1), jnp.maximum(s2, s4)), axis=-1, keepdims=True)
            pa = jnp.concatenate([jnp.exp(s0 - top).astype(BF), jnp.exp(s1 - top).astype(BF)], axis=1)
            pb = jnp.concatenate([jnp.exp(s2 - top).astype(BF), jnp.exp(s4 - top).astype(BF)], axis=1)
            va = jnp.concatenate([jnp.concatenate([kvo[:, v], kvc[:, v]], axis=0), ones], axis=1)
            vb = jnp.concatenate([jnp.concatenate([kv2[:, v] if kv2 is not None else blank, kv4[:, v] if kv4 is not None else blank], axis=0), ones], axis=1)
            r = jnp.dot(pa, va, preferred_element_type=F32) + jnp.dot(pb, vb, preferred_element_type=F32)
            num = jnp.where(low, r[:R, :128], r[R:, :128])
            den = jnp.where(low, r[:R, 128:], r[R:, 128:])
            att_s[:, o] = (num / den).astype(BF)

        hid_s[...] = x_s[0:R, :].astype(F32) + jnp.dot(att_s[...], wout[...], preferred_element_type=F32)
        hid = hid_s[...]
        lifted = (hid * rms_scale(hid) * g2[...]).astype(BF)
        for j in range(2):
            up = jnp.dot(lifted, wup[:, j * D:(j + 1) * D], preferred_element_type=F32)
            act_s[:, j * D:(j + 1) * D] = jax.nn.gelu(up).astype(BF)
        out = (hid_s[...] + jnp.dot(act_s[...], wdown[...], preferred_element_type=F32)).astype(BF)
        out_ref[0:R, :] = out
        out_ref[R:, :] = h_s[...]
        if last_possible:
            @pl.when(stage == STAGES - 1)
            def _():
                y = out_ref[0:R, :].astype(F32)
                logits = jnp.sum(y * rms_scale(y) * whead[...], axis=-1, keepdims=True)
                spin = shifted_column(spin_row(spins, sample, b), None, False)
                terms = math.log(2.0) - jax.nn.softplus((1.0 - 2.0 * spin) * logits)
                i = lax.broadcasted_iota(jnp.int32, (R, R), 0)
                j = lax.broadcasted_iota(jnp.int32, (R, R), 1)
                cum = jnp.sum(jnp.where(i <= j, terms, 0.0), axis=0, keepdims=True)
                tot = jnp.sum(jnp.broadcast_to(terms, (R, R)), axis=0, keepdims=True)
                run = run_in[1:2, :] if run_in is not None else jnp.zeros((1, 128), F32)
                msg[...] = jnp.concatenate([cum + run, tot + run, jnp.zeros((6, 128), F32)], axis=0)


def layer_call(k, args):
    vm = pl.BlockSpec(memory_space=pltpu.VMEM)
    shapes = [jax.ShapeDtypeStruct((R + H, D), BF), jax.ShapeDtypeStruct((R, 2 * D), BF)]
    if k >= 2 * (STAGES - 1):
        shapes.append(jax.ShapeDtypeStruct((8, 128), F32))
    return pl.pallas_call(
        functools.partial(layer_kernel, k=k),
        out_shape=tuple(shapes),
        in_specs=[vm] * len(args),
        out_specs=(vm,) * len(shapes),
        scratch_shapes=[
            pltpu.VMEM((2 * R, D), BF),
            pltpu.VMEM((H, D), BF),
            pltpu.VMEM((R, 2 * D), BF),
            pltpu.VMEM((R, D), BF),
            pltpu.VMEM((R, D), BF),
            pltpu.VMEM((R, D), F32),
            pltpu.VMEM((R, FF), BF),
        ],
        compiler_params=pltpu.CompilerParams(vmem_limit_bytes=20 << 20),
        cost_estimate=pl.CostEstimate(flops=4 * 10**9, bytes_accessed=10**6, transcendentals=10**6),
        name=f"layer{k}",
    )(*args)


def senders_at(k):
    for end, stages in ((8, (0, 1, 2, 3)), (20, (1, 2, 3, 4, 5, 6))):
        if k < end:
            return stages
    return ()


def body(spins, block_mask, tok_embed, pos_embed, norm1_gain, w_qkv, w_out, norm2_gain, w_up, w_down, w_head):
    def send(value, pairs):
        return lax.ppermute(value, AX, pairs)

    first_own = send(pos_embed, [(dev(s, p), dev(0, 2 * s + p)) for s in range(STAGES) for p in range(2)])
    first_copy = send(pos_embed, [(dev(s, 0), dev(0, 2 * s + 1)) for s in range(STAGES)])
    behind = send(pos_embed, [(dev(s, c), dev(s, c + 1)) for s in range(STAGES) for c in range(CTX - 1)])
    weights = (w_qkv[0], w_out[0], w_up[0], w_down[0])
    double = feed_call(block_mask, pos_embed, behind)
    rest = weights + (norm1_gain, norm2_gain, tok_embed, w_head[None], spins)

    def feed(m):
        return send(double, [(dev(s, 2 * m + p), dev(0, 2 * s + p)) for s in range(STAGES) for p in range(2)])

    feeds = {m: feed(m) for m in range(1, 4)}
    kvs, owns, copies = {}, {}, {}
    run, result = None, None
    for k in range(TICKS):
        args = []
        if k == 0:
            args += [first_own, first_copy]
        elif k < MICRO:
            args.append(feeds[k])
        if k >= 2:
            args += [owns[k - 2], copies[max(k - 3, 0)], copies[k - 2]]
        args += [kvs[j] for j in (k - 1, k - 2) if j >= 0]
        args += rest
        if run is not None:
            args.append(run)
        outs = layer_call(k, args)
        out, kvs[k] = outs[0], outs[1]
        senders = senders_at(k)
        if senders:
            owns[k] = send(out, [(dev(s, c), dev(s + 1, c)) for s in senders for c in range(CTX)])
            copies[k] = send(out, [(dev(s, c), dev(s + 1, c ^ 1)) for s in senders for c in range(CTX)])
        if k == 0:
            double, _ = lax.optimization_barrier((double, out))
            for m in range(4, MICRO):
                feeds[m] = feed(m)
        if k >= 2 * (STAGES - 1):
            m = k - 2 * (STAGES - 1)
            run = outs[2]
            a = send(run, [(dev(STAGES - 1, 2 * n + p), dev(n, 2 * m + p)) for n in range(STAGES) for p in range(2)])
            z = send(
                run,
                [
                    (dev(STAGES - 1, 2 * n + p), dev(n, 2 * m + p + 1))
                    for n in range(STAGES)
                    for p in range(2)
                    if 2 * m + p + 1 < CTX
                ],
            )
            part = a[0:1] + z[1:2]
            result = part if result is None else result + part
    return 0.5 * result


def solution(mesh):
    return jax.shard_map(
        body,
        mesh=mesh,
        in_specs=(
            P(),
            P("ctx", None),
            P(),
            P("ctx", None),
            P("section", None),
            P("section", None, None),
            P("section", None, None),
            P("section", None),
            P("section", None, None),
            P("section", None, None),
            P(),
        ),
        out_specs=P("section", "ctx"),
        check_vma=False,
    )
```

```python
import functools
import math

import jax
import jax.numpy as jnp
from jax import lax
from jax.experimental import pallas as pl
from jax.experimental.pallas import tpu as pltpu
from jax.sharding import PartitionSpec as P

F32, BF = jnp.float32, jnp.bfloat16
R = 128
H = 8
D, FF = 1024, 2048
PAIRS = 8
STAGES, CTX, MICRO = 8, 16, 8
TICKS = MICRO + 2 * (STAGES - 1)
NEG = -1e30
AX = ("section", "ctx")


def dev(s, c):
    return s * CTX + c


def rms_scale(v):
    return lax.rsqrt(jnp.mean(v * v, axis=-1, keepdims=True) + 1e-05)


def shifted_column(row, before, shift):
    i = lax.broadcasted_iota(jnp.int32, (R, R), 0)
    j = lax.broadcasted_iota(jnp.int32, (R, R), 1)
    if not shift:
        return jnp.sum(jnp.where(i == j, row, 0.0), axis=1, keepdims=True)
    both = jnp.where(i == j + 1, row, 0.0) + jnp.where((i == 0) & (j == R - 1), before, 0.0)
    return jnp.sum(both, axis=1, keepdims=True)


def spin_row(spins, sample, block):
    start = pl.multiple_of(jnp.maximum(block, 0) * R, R)
    rows = spins[:, pl.ds(start, R)].astype(F32)
    return jnp.sum(jnp.where(lax.broadcasted_iota(jnp.int32, rows.shape, 0) == sample, rows, 0.0), axis=0, keepdims=True)


def load_kernel(*refs):
    sem = refs[-1]
    half = len(refs) // 2
    copies = [pltpu.make_async_copy(refs[i], refs[half + i], sem.at[i]) for i in range(half)]
    for copy in copies:
        copy.start()
    for copy in copies:
        copy.wait()


def load_call(values):
    return pl.pallas_call(
        load_kernel,
        out_shape=tuple(pltpu.VMEM(v.shape, v.dtype) for v in values),
        in_specs=[pl.BlockSpec(memory_space=pltpu.HBM)] * len(values),
        out_specs=(pl.BlockSpec(memory_space=pltpu.VMEM),) * len(values),
        scratch_shapes=[pltpu.SemaphoreType.DMA((len(values),))],
        compiler_params=pltpu.CompilerParams(vmem_limit_bytes=4 << 20),
        cost_estimate=pl.CostEstimate(flops=5 * 10**9, bytes_accessed=32 << 20, transcendentals=0),
        name="load",
    )(*(pltpu.with_memory_space_constraint(v, pltpu.HBM) for v in values))


def feed_kernel(mask, pos, behind, out):
    ctx = lax.axis_index("ctx")
    out[0:R, :] = pos[...]
    out[R + H:, :] = behind[...]
    columns = lax.broadcasted_iota(jnp.int32, (1, 128), 1)
    row = mask[...]
    flags = []
    for distance in (1, 2, 4):
        at = lax.broadcasted_iota(jnp.int32, (1, CTX), 1)
        hit = jnp.sum(jnp.where((at == ctx - distance) & (row == 1), 1.0, 0.0), axis=1, keepdims=True)
        flags.append(jnp.broadcast_to(hit, (H, 128)))
    flags.append(jnp.zeros((H, D - 384), F32))
    out[R:R + H, :] = jnp.concatenate(flags, axis=1).astype(BF)


def feed_call(mask, pos, behind):
    vm = pl.BlockSpec(memory_space=pltpu.VMEM)
    return pl.pallas_call(
        feed_kernel,
        out_shape=jax.ShapeDtypeStruct((2 * R + H, D), BF),
        in_specs=[vm] * 3,
        out_specs=vm,
        compiler_params=pltpu.CompilerParams(vmem_limit_bytes=4 << 20),
        name="feed",
    )(mask, pos, behind)


def layer_kernel(*refs, k):
    it = iter(refs)
    first = [next(it) for _ in range(2)] if k == 0 else None
    e_ref = next(it) if 0 < k < MICRO else None
    has_o = k >= 2
    o_ref, ca_ref, cb_ref = (next(it), next(it), next(it)) if has_o else (None, None, None)
    kv2 = next(it) if k >= 1 else None
    kv4 = next(it) if k >= 2 else None
    last_possible = k >= 2 * (STAGES - 1)
    wqkv, wout, wup, wdown, g1, g2, tok, whead, spins = [next(it) for _ in range(9)]
    msg_in = next(it) if k > 2 * (STAGES - 1) else None
    out_ref, kvo = next(it), next(it)
    msg = next(it) if last_possible else None
    x_s, h_s, kvc, q_s, att_s, hid_s, act_s = [next(it) for _ in range(7)]
    stage, ctx = lax.axis_index("section"), lax.axis_index("ctx")
    sample, odd = ctx // 2, ctx % 2
    m = k - 2 * stage
    b = 2 * m + odd

    if k < 2 * (STAGES - 1):
        @pl.when((m == -1) | (m == -2))
        def _():
            kvo[...] = jnp.zeros_like(kvo)

    @pl.when((m >= 0) & (m < MICRO))
    def _():
        if k < MICRO:
            @pl.when(stage == 0)
            def _():
                def embed(block, pos):
                    before = jnp.where(block > 0, spin_row(spins, sample, block - 1), 2.0)
                    t = shifted_column(spin_row(spins, sample, block), before, True)
                    rows = jnp.where(t == 0.0, tok[0:1, :], jnp.where(t == 1.0, tok[1:2, :], tok[2:3, :]))
                    return (rows + pos.astype(F32)).astype(BF)

                if k == 0:
                    x_s[0:R, :] = embed(b, first[0][...])
                    x_s[R:, :] = embed(b - 1, first[1][...])
                    lanes = lax.broadcasted_iota(jnp.int32, (H, D), 1)
                    h_s[...] = jnp.where((lanes < 128) & (odd == 1), 1.0, 0.0).astype(BF)
                else:
                    x_s[0:R, :] = embed(b, e_ref[0:R, :])
                    x_s[R:, :] = embed(b - 1, e_ref[R + H:2 * R + H, :])
                    h_s[...] = e_ref[R:R + H, :]
        if has_o:
            @pl.when(stage > 0)
            def _():
                x_s[0:R, :] = o_ref[0:R, :]
                h_s[...] = o_ref[R:R + H, :]

                @pl.when(odd == 0)
                def _():
                    x_s[R:, :] = ca_ref[0:R, :]

                @pl.when(odd == 1)
                def _():
                    x_s[R:, :] = cb_ref[0:R, :]

        xf = x_s[...].astype(F32)
        a = (xf * rms_scale(xf) * g1[...]).astype(BF)
        q_s[...] = (jnp.dot(a[0:R, :], wqkv[:, :D], preferred_element_type=F32) * 0.125).astype(BF)
        for j in range(2):
            p = jnp.dot(a, wqkv[:, (j + 1) * D:(j + 2) * D], preferred_element_type=F32).astype(BF)
            kvo[:, j * D:(j + 1) * D] = p[:R]
            kvc[:, j * D:(j + 1) * D] = p[R:]

        lane = lax.broadcasted_iota(jnp.int32, (R, 128), 1)
        row = lax.broadcasted_iota(jnp.int32, (R, 128), 0)
        causal = jnp.where(lane <= row, 0.0, NEG)
        causal2 = jnp.concatenate([causal, causal], axis=0)
        flags = h_s[0:1, 0:384].astype(F32)
        f1, f2, f4 = [jnp.where(flags[:, i * 128:(i + 1) * 128] > 0.5, 0.0, NEG) for i in range(3)]
        ones = jnp.ones((2 * R, 128), BF)
        low = lane < 64
        nt = (((1,), (1,)), ((), ()))
        for h in range(PAIRS):
            o, v = slice(h * 128, h * 128 + 128), slice(D + h * 128, D + h * 128 + 128)
            q = q_s[:, o]
            zero = jnp.zeros_like(q)
            q2 = jnp.concatenate([jnp.where(low, q, zero), jnp.where(low, zero, q)], axis=0)
            ka = jnp.concatenate([kvo[:, o], kvc[:, o]], axis=0)
            blank = jnp.zeros((R, 128), BF)
            kb = jnp.concatenate([kv2[:, o] if kv2 is not None else blank, kv4[:, o] if kv4 is not None else blank], axis=0)
            sa = lax.dot_general(q2, ka, nt, preferred_element_type=F32)
            sb = lax.dot_general(q2, kb, nt, preferred_element_type=F32)
            s0 = sa[:, :128] + causal2
            s1 = sa[:, 128:] + f1
            s2 = sb[:, :128] + f2
            s4 = sb[:, 128:] + f4
            top = jnp.max(jnp.maximum(jnp.maximum(s0, s1), jnp.maximum(s2, s4)), axis=-1, keepdims=True)
            pa = jnp.concatenate([jnp.exp(s0 - top).astype(BF), jnp.exp(s1 - top).astype(BF)], axis=1)
            pb = jnp.concatenate([jnp.exp(s2 - top).astype(BF), jnp.exp(s4 - top).astype(BF)], axis=1)
            va = jnp.concatenate([jnp.concatenate([kvo[:, v], kvc[:, v]], axis=0), ones], axis=1)
            vb = jnp.concatenate([jnp.concatenate([kv2[:, v] if kv2 is not None else blank, kv4[:, v] if kv4 is not None else blank], axis=0), ones], axis=1)
            r = jnp.dot(pa, va, preferred_element_type=F32) + jnp.dot(pb, vb, preferred_element_type=F32)
            num = jnp.where(low, r[:R, :128], r[R:, :128])
            den = jnp.where(low, r[:R, 128:], r[R:, 128:])
            att_s[:, o] = (num / den).astype(BF)

        hid_s[...] = x_s[0:R, :].astype(F32) + jnp.dot(att_s[...], wout[...], preferred_element_type=F32)
        hid = hid_s[...]
        lifted = (hid * rms_scale(hid) * g2[...]).astype(BF)
        for j in range(2):
            up = jnp.dot(lifted, wup[:, j * D:(j + 1) * D], preferred_element_type=F32)
            act_s[:, j * D:(j + 1) * D] = jax.nn.gelu(up).astype(BF)
        out = (hid_s[...] + jnp.dot(act_s[...], wdown[...], preferred_element_type=F32)).astype(BF)
        out_ref[0:R, :] = out
        out_ref[R:, :] = h_s[...]
        t0 = k - 2 * (STAGES - 1)
        if last_possible:
            @pl.when(stage == STAGES - 1)
            def _():
                y = out_ref[0:R, :].astype(F32)
                logits = jnp.sum(y * rms_scale(y) * whead[...], axis=-1, keepdims=True)
                spin = shifted_column(spin_row(spins, sample, b), None, False)
                terms = math.log(2.0) - jax.nn.softplus((1.0 - 2.0 * spin) * logits)
                i = lax.broadcasted_iota(jnp.int32, (R, R), 0)
                j = lax.broadcasted_iota(jnp.int32, (R, R), 1)
                cum = jnp.sum(jnp.where(i <= j, terms, 0.0), axis=0, keepdims=True)
                tot = jnp.sum(jnp.broadcast_to(terms, (R, R)), axis=0, keepdims=True)
                if msg_in is None:
                    run = jnp.zeros((1, 128), F32)
                    msg[8:, :] = jnp.zeros((8 * MICRO - 8, 128), F32)
                else:
                    msg[...] = msg_in[...]
                    run = msg_in[8 * t0 - 8:8 * t0, :][1:2, :]
                msg[8 * t0:8 * t0 + 8, :] = jnp.concatenate([cum + run, tot + run, jnp.zeros((6, 128), F32)], axis=0)


def scatter_kernel(msg, out):
    stage, ctx = lax.axis_index("section"), lax.axis_index("ctx")
    out[...] = jnp.zeros_like(out)

    @pl.when(stage == STAGES - 1)
    def _():
        odd = ctx % 2
        base = (ctx // 2) * CTX
        zero = jnp.zeros((1, 128), F32)
        for j in range(CTX):
            own = msg[(j // 2) * 8:(j // 2) * 8 + 8, :]
            start = pl.multiple_of((base + j) * 8, 8)
            past = (j - 1) // 2
            other = msg[past * 8:past * 8 + 8, :][1:2, :] if j > 0 else zero
            same = odd == j % 2
            tile = jnp.concatenate([jnp.where(same, own[0:1, :], 0.0), jnp.where(same, 0.0, other), jnp.zeros((6, 128), F32)], axis=0)
            out[pl.ds(start, 8), :] = tile


def gather_kernel(got, out):
    stage = lax.axis_index("section")
    base = ((STAGES - 1) * CTX + 2 * stage) * 8
    even = got[pl.ds(pl.multiple_of(base, 8), 8), :]
    odd = got[pl.ds(pl.multiple_of(base + 8, 8), 8), :]
    both = even + odd
    out[...] = 0.5 * (both[0:1, :] + both[1:2, :])


def small_call(kernel, shape, arg):
    vm = pl.BlockSpec(memory_space=pltpu.VMEM)
    return pl.pallas_call(
        kernel,
        out_shape=jax.ShapeDtypeStruct(shape, F32),
        in_specs=[vm],
        out_specs=vm,
        compiler_params=pltpu.CompilerParams(vmem_limit_bytes=8 << 20),
    )(arg)


def layer_call(k, args):
    vm = pl.BlockSpec(memory_space=pltpu.VMEM)
    shapes = [jax.ShapeDtypeStruct((R + H, D), BF), jax.ShapeDtypeStruct((R, 2 * D), BF)]
    if k >= 2 * (STAGES - 1):
        shapes.append(jax.ShapeDtypeStruct((8 * MICRO, 128), F32))
    return pl.pallas_call(
        functools.partial(layer_kernel, k=k),
        out_shape=tuple(shapes),
        in_specs=[vm] * len(args),
        out_specs=(vm,) * len(shapes),
        scratch_shapes=[
            pltpu.VMEM((2 * R, D), BF),
            pltpu.VMEM((H, D), BF),
            pltpu.VMEM((R, 2 * D), BF),
            pltpu.VMEM((R, D), BF),
            pltpu.VMEM((R, D), BF),
            pltpu.VMEM((R, D), F32),
            pltpu.VMEM((R, FF), BF),
        ],
        compiler_params=pltpu.CompilerParams(vmem_limit_bytes=20 << 20),
        cost_estimate=pl.CostEstimate(flops=4 * 10**9, bytes_accessed=10**6, transcendentals=10**6),
    )(*args)


def senders_at(k):
    return (0, 1, 2, 3) if k < 8 else (1, 2, 3, 4, 5, 6) if k < 20 else ()


def program(spins, block_mask, tok_embed, pos_embed, norm1_gain, w_qkv, w_out, norm2_gain, w_up, w_down, w_head):
    def send(value, pairs):
        return lax.ppermute(value, AX, pairs)

    first_own = send(pos_embed, [(dev(s, p), dev(0, 2 * s + p)) for s in range(STAGES) for p in range(2)])
    first_copy = send(pos_embed, [(dev(s, 0), dev(0, 2 * s + 1)) for s in range(STAGES)])
    behind = send(pos_embed, [(dev(s, c), dev(s, c + 1)) for s in range(STAGES) for c in range(CTX - 1)])
    loaded = load_call(
        (w_qkv[0], w_out[0], w_up[0], w_down[0], norm1_gain, norm2_gain, tok_embed, w_head[None], spins, pos_embed, block_mask)
    )
    rest, (pos, mask) = loaded[:9], loaded[9:]
    double = feed_call(mask, pos, behind)

    def feed(m):
        return send(double, [(dev(s, 2 * m + p), dev(0, 2 * s + p)) for s in range(STAGES) for p in range(2)])

    feeds = {m: feed(m) for m in range(1, 4)}
    kvs, owns, to_odd, to_even = {}, {}, {}, {}
    messages = None
    for k in range(TICKS):
        args = []
        if k == 0:
            args += [first_own, first_copy]
        elif k < MICRO:
            args.append(feeds[k])
        if k >= 2:
            args += [owns[k - 2], to_even[max(k - 3, 0)], to_odd[k - 2]]
        args += [kvs[j] for j in (k - 1, k - 2) if j >= 0]
        args += rest
        if messages is not None:
            args.append(messages)
        outs = layer_call(k, args)
        out, kvs[k] = outs[0], outs[1]
        if k >= 2 * (STAGES - 1):
            messages = outs[2]
        senders = senders_at(k)
        if senders:
            owns[k] = send(out, [(dev(s, c), dev(s + 1, c)) for s in senders for c in range(CTX)])
            to_odd[k] = send(out, [(dev(s, c), dev(s + 1, c + 1)) for s in senders for c in range(0, CTX, 2)])
            to_even[k] = send(out, [(dev(s, c), dev(s + 1, c - 1)) for s in senders for c in range(1, CTX, 2)])
        if k == 0:
            double, _ = lax.optimization_barrier((double, out))
            for m in range(4, MICRO):
                feeds[m] = feed(m)
    tiles = small_call(scatter_kernel, (STAGES * CTX * 8, 128), messages)
    got = lax.all_to_all(tiles.reshape(STAGES * CTX, 8, 128), AX, 0, 0, tiled=True)
    return small_call(gather_kernel, (1, 128), got.reshape(STAGES * CTX * 8, 128))


def solution(mesh):
    return jax.shard_map(
        program,
        mesh=mesh,
        in_specs=(
            P(),
            P("ctx", None),
            P(),
            P("ctx", None),
            P("section", None),
            P("section", None, None),
            P("section", None, None),
            P("section", None),
            P("section", None, None),
            P("section", None, None),
            P(),
        ),
        out_specs=P("section", "ctx"),
        check_vma=False,
    )
```

```python
import functools
import math

import jax
import jax.numpy as jnp
from jax import lax
from jax.experimental import pallas as pl
from jax.experimental.pallas import tpu as pltpu
from jax.sharding import PartitionSpec as P

F32, BF = jnp.float32, jnp.bfloat16
R = 128
H = 8
D, FF = 1024, 2048
PAIRS = 8
STAGES, CTX, MICRO = 8, 16, 8
TICKS = MICRO + 2 * (STAGES - 1)
NEG = -1e30
AX = ("section", "ctx")


def dev(s, c):
    return s * CTX + c


def rms_scale(v):
    return lax.rsqrt(jnp.mean(v * v, axis=-1, keepdims=True) + 1e-05)


def shifted_column(row, before, shift):
    i = lax.broadcasted_iota(jnp.int32, (R, R), 0)
    j = lax.broadcasted_iota(jnp.int32, (R, R), 1)
    if not shift:
        return jnp.sum(jnp.where(i == j, row, 0.0), axis=1, keepdims=True)
    both = jnp.where(i == j + 1, row, 0.0) + jnp.where((i == 0) & (j == R - 1), before, 0.0)
    return jnp.sum(both, axis=1, keepdims=True)


def spin_row(spins, sample, block):
    start = pl.multiple_of(jnp.maximum(block, 0) * R, R)
    rows = spins[:, pl.ds(start, R)].astype(F32)
    return jnp.sum(jnp.where(lax.broadcasted_iota(jnp.int32, rows.shape, 0) == sample, rows, 0.0), axis=0, keepdims=True)


def load_kernel(*refs):
    sem = refs[-1]
    half = len(refs) // 2
    copies = [pltpu.make_async_copy(refs[i], refs[half + i], sem.at[i]) for i in range(half)]
    for copy in copies:
        copy.start()
    for copy in copies:
        copy.wait()


def load_call(values):
    return pl.pallas_call(
        load_kernel,
        out_shape=tuple(pltpu.VMEM(v.shape, v.dtype) for v in values),
        in_specs=[pl.BlockSpec(memory_space=pltpu.HBM)] * len(values),
        out_specs=(pl.BlockSpec(memory_space=pltpu.VMEM),) * len(values),
        scratch_shapes=[pltpu.SemaphoreType.DMA((len(values),))],
        compiler_params=pltpu.CompilerParams(vmem_limit_bytes=4 << 20),
        cost_estimate=pl.CostEstimate(flops=5 * 10**9, bytes_accessed=32 << 20, transcendentals=0),
        name="load",
    )(*(pltpu.with_memory_space_constraint(v, pltpu.HBM) for v in values))


def feed_kernel(mask, pos, behind, out):
    ctx = lax.axis_index("ctx")
    out[0:R, :] = pos[...]
    out[R + H:, :] = behind[...]
    columns = lax.broadcasted_iota(jnp.int32, (1, 128), 1)
    row = mask[...]
    flags = []
    for distance in (1, 2, 4):
        at = lax.broadcasted_iota(jnp.int32, (1, CTX), 1)
        hit = jnp.sum(jnp.where((at == ctx - distance) & (row == 1), 1.0, 0.0), axis=1, keepdims=True)
        flags.append(jnp.broadcast_to(hit, (H, 128)))
    flags.append(jnp.zeros((H, D - 384), F32))
    out[R:R + H, :] = jnp.concatenate(flags, axis=1).astype(BF)


def feed_call(mask, pos, behind):
    vm = pl.BlockSpec(memory_space=pltpu.VMEM)
    return pl.pallas_call(
        feed_kernel,
        out_shape=jax.ShapeDtypeStruct((2 * R + H, D), BF),
        in_specs=[vm] * 3,
        out_specs=vm,
        compiler_params=pltpu.CompilerParams(vmem_limit_bytes=4 << 20),
        name="feed",
    )(mask, pos, behind)


def layer_kernel(*refs, k):
    it = iter(refs)
    first = [next(it) for _ in range(2)] if k == 0 else None
    e_ref = next(it) if 0 < k < MICRO else None
    has_o = k >= 2
    o_ref, ca_ref, cb_ref = (next(it), next(it), next(it)) if has_o else (None, None, None)
    kv2 = next(it) if k >= 1 else None
    kv4 = next(it) if k >= 2 else None
    last_possible = k >= 2 * (STAGES - 1)
    wqkv, wout, wup, wdown, g1, g2, tok, whead, spins = [next(it) for _ in range(9)]
    msg_in = next(it) if k > 2 * (STAGES - 1) else None
    out_ref, kvo = next(it), next(it)
    msg = next(it) if last_possible else None
    x_s, h_s, kvc, q_s, att_s, hid_s, act_s = [next(it) for _ in range(7)]
    stage, ctx = lax.axis_index("section"), lax.axis_index("ctx")
    sample, odd = ctx // 2, ctx % 2
    m = k - 2 * stage
    b = 2 * m + odd

    if k < 2 * (STAGES - 1):
        @pl.when((m == -1) | (m == -2))
        def _():
            kvo[...] = jnp.zeros_like(kvo)

    @pl.when((m >= 0) & (m < MICRO))
    def _():
        if k < MICRO:
            @pl.when(stage == 0)
            def _():
                def embed(block, pos):
                    before = jnp.where(block > 0, spin_row(spins, sample, block - 1), 2.0)
                    t = shifted_column(spin_row(spins, sample, block), before, True)
                    rows = jnp.where(t == 0.0, tok[0:1, :], jnp.where(t == 1.0, tok[1:2, :], tok[2:3, :]))
                    return (rows + pos.astype(F32)).astype(BF)

                if k == 0:
                    x_s[0:R, :] = embed(b, first[0][...])
                    x_s[R:, :] = embed(b - 1, first[1][...])
                    lanes = lax.broadcasted_iota(jnp.int32, (H, D), 1)
                    h_s[...] = jnp.where((lanes < 128) & (odd == 1), 1.0, 0.0).astype(BF)
                else:
                    x_s[0:R, :] = embed(b, e_ref[0:R, :])
                    x_s[R:, :] = embed(b - 1, e_ref[R + H:2 * R + H, :])
                    h_s[...] = e_ref[R:R + H, :]
        if has_o:
            @pl.when(stage > 0)
            def _():
                x_s[0:R, :] = o_ref[0:R, :]
                h_s[...] = o_ref[R:R + H, :]

                @pl.when(odd == 0)
                def _():
                    x_s[R:, :] = ca_ref[0:R, :]

                @pl.when(odd == 1)
                def _():
                    x_s[R:, :] = cb_ref[0:R, :]

        xf = x_s[...].astype(F32)
        a = (xf * rms_scale(xf) * g1[...]).astype(BF)
        q_s[...] = (jnp.dot(a[0:R, :], wqkv[:, :D], preferred_element_type=F32) * 0.125).astype(BF)
        for j in range(2):
            p = jnp.dot(a, wqkv[:, (j + 1) * D:(j + 2) * D], preferred_element_type=F32).astype(BF)
            kvo[:, j * D:(j + 1) * D] = p[:R]
            kvc[:, j * D:(j + 1) * D] = p[R:]

        lane = lax.broadcasted_iota(jnp.int32, (R, 128), 1)
        row = lax.broadcasted_iota(jnp.int32, (R, 128), 0)
        causal = jnp.where(lane <= row, 0.0, NEG)
        causal2 = jnp.concatenate([causal, causal], axis=0)
        flags = h_s[0:1, 0:384].astype(F32)
        f1, f2, f4 = [jnp.where(flags[:, i * 128:(i + 1) * 128] > 0.5, 0.0, NEG) for i in range(3)]
        ones = jnp.ones((2 * R, 128), BF)
        low = lane < 64
        nt = (((1,), (1,)), ((), ()))
        for h in range(PAIRS):
            o, v = slice(h * 128, h * 128 + 128), slice(D + h * 128, D + h * 128 + 128)
            q = q_s[:, o]
            zero = jnp.zeros_like(q)
            q2 = jnp.concatenate([jnp.where(low, q, zero), jnp.where(low, zero, q)], axis=0)
            ka = jnp.concatenate([kvo[:, o], kvc[:, o]], axis=0)
            blank = jnp.zeros((R, 128), BF)
            kb = jnp.concatenate([kv2[:, o] if kv2 is not None else blank, kv4[:, o] if kv4 is not None else blank], axis=0)
            sa = lax.dot_general(q2, ka, nt, preferred_element_type=F32)
            sb = lax.dot_general(q2, kb, nt, preferred_element_type=F32)
            s0 = sa[:, :128] + causal2
            s1 = sa[:, 128:] + f1
            s2 = sb[:, :128] + f2
            s4 = sb[:, 128:] + f4
            top = jnp.max(jnp.maximum(jnp.maximum(s0, s1), jnp.maximum(s2, s4)), axis=-1, keepdims=True)
            pa = jnp.concatenate([jnp.exp(s0 - top).astype(BF), jnp.exp(s1 - top).astype(BF)], axis=1)
            pb = jnp.concatenate([jnp.exp(s2 - top).astype(BF), jnp.exp(s4 - top).astype(BF)], axis=1)
            va = jnp.concatenate([jnp.concatenate([kvo[:, v], kvc[:, v]], axis=0), ones], axis=1)
            vb = jnp.concatenate([jnp.concatenate([kv2[:, v] if kv2 is not None else blank, kv4[:, v] if kv4 is not None else blank], axis=0), ones], axis=1)
            r = jnp.dot(pa, va, preferred_element_type=F32) + jnp.dot(pb, vb, preferred_element_type=F32)
            num = jnp.where(low, r[:R, :128], r[R:, :128])
            den = jnp.where(low, r[:R, 128:], r[R:, 128:])
            att_s[:, o] = (num / den).astype(BF)

        hid_s[...] = x_s[0:R, :].astype(F32) + jnp.dot(att_s[...], wout[...], preferred_element_type=F32)
        hid = hid_s[...]
        lifted = (hid * rms_scale(hid) * g2[...]).astype(BF)
        for j in range(2):
            up = jnp.dot(lifted, wup[:, j * D:(j + 1) * D], preferred_element_type=F32)
            act_s[:, j * D:(j + 1) * D] = jax.nn.gelu(up).astype(BF)
        out = (hid_s[...] + jnp.dot(act_s[...], wdown[...], preferred_element_type=F32)).astype(BF)
        out_ref[0:R, :] = out
        out_ref[R:, :] = h_s[...]
        if last_possible:
            @pl.when(stage == STAGES - 1)
            def _():
                y = out_ref[0:R, :].astype(F32)
                logits = jnp.sum(y * rms_scale(y) * whead[...], axis=-1, keepdims=True)
                spin = shifted_column(spin_row(spins, sample, b), None, False)
                terms = math.log(2.0) - jax.nn.softplus((1.0 - 2.0 * spin) * logits)
                i = lax.broadcasted_iota(jnp.int32, (R, R), 0)
                j = lax.broadcasted_iota(jnp.int32, (R, R), 1)
                cum = jnp.sum(jnp.where(i <= j, terms, 0.0), axis=0, keepdims=True)
                tot = jnp.sum(jnp.broadcast_to(terms, (R, R)), axis=0, keepdims=True)
                run = jnp.zeros((1, 128), F32) if msg_in is None else msg_in[1:2, :]
                msg[...] = jnp.concatenate([cum + run, tot + run, run, jnp.zeros((5, 128), F32)], axis=0)


def keep_kernel(*refs):
    stage = lax.axis_index("section")
    for m in range(MICRO):
        @pl.when(stage == m)
        def _():
            refs[-1][...] = refs[m][...]


def keep_call(parts):
    vm = pl.BlockSpec(memory_space=pltpu.VMEM)
    return pl.pallas_call(
        keep_kernel,
        out_shape=jax.ShapeDtypeStruct((8, 128), F32),
        in_specs=[vm] * MICRO,
        out_specs=vm,
        compiler_params=pltpu.CompilerParams(vmem_limit_bytes=4 << 20),
        name="keep",
    )(*parts)


def merge_kernel(own, other, out):
    odd = lax.axis_index("ctx") % 2
    out[...] = 0.5 * (own[0:1, :] + jnp.where(odd == 1, other[1:2, :], other[2:3, :]))


def merge_call(own, other):
    vm = pl.BlockSpec(memory_space=pltpu.VMEM)
    return pl.pallas_call(
        merge_kernel,
        out_shape=jax.ShapeDtypeStruct((1, 128), F32),
        in_specs=[vm, vm],
        out_specs=vm,
        compiler_params=pltpu.CompilerParams(vmem_limit_bytes=4 << 20),
        name="merge",
    )(own, other)


def layer_call(k, args):
    vm = pl.BlockSpec(memory_space=pltpu.VMEM)
    shapes = [jax.ShapeDtypeStruct((R + H, D), BF), jax.ShapeDtypeStruct((R, 2 * D), BF)]
    if k >= 2 * (STAGES - 1):
        shapes.append(jax.ShapeDtypeStruct((8, 128), F32))
    return pl.pallas_call(
        functools.partial(layer_kernel, k=k),
        out_shape=tuple(shapes),
        in_specs=[vm] * len(args),
        out_specs=(vm,) * len(shapes),
        scratch_shapes=[
            pltpu.VMEM((2 * R, D), BF),
            pltpu.VMEM((H, D), BF),
            pltpu.VMEM((R, 2 * D), BF),
            pltpu.VMEM((R, D), BF),
            pltpu.VMEM((R, D), BF),
            pltpu.VMEM((R, D), F32),
            pltpu.VMEM((R, FF), BF),
        ],
        compiler_params=pltpu.CompilerParams(vmem_limit_bytes=20 << 20),
        cost_estimate=pl.CostEstimate(flops=4 * 10**9, bytes_accessed=10**6, transcendentals=10**6),
    )(*args)


def senders_at(k):
    return (0, 1, 2, 3) if k < 8 else (1, 2, 3, 4, 5, 6) if k < 20 else ()


def program(spins, block_mask, tok_embed, pos_embed, norm1_gain, w_qkv, w_out, norm2_gain, w_up, w_down, w_head):
    def send(value, pairs):
        return lax.ppermute(value, AX, pairs)

    first_own = send(pos_embed, [(dev(s, p), dev(0, 2 * s + p)) for s in range(STAGES) for p in range(2)])
    first_copy = send(pos_embed, [(dev(s, 0), dev(0, 2 * s + 1)) for s in range(STAGES)])
    behind = send(pos_embed, [(dev(s, c), dev(s, c + 1)) for s in range(STAGES) for c in range(CTX - 1)])
    loaded = load_call(
        (w_qkv[0], w_out[0], w_up[0], w_down[0], norm1_gain, norm2_gain, tok_embed, w_head[None], spins, pos_embed, block_mask)
    )
    rest, (pos, mask) = loaded[:9], loaded[9:]
    double = feed_call(mask, pos, behind)

    def feed(m):
        return send(double, [(dev(s, 2 * m + p), dev(0, 2 * s + p)) for s in range(STAGES) for p in range(2)])

    feeds = {m: feed(m) for m in range(1, MICRO)}
    kvs, owns, to_odd, to_even = {}, {}, {}, {}
    last = STAGES - 1
    run, parts = None, []
    for k in range(TICKS):
        args = []
        if k == 0:
            args += [first_own, first_copy]
        elif k < MICRO:
            args.append(feeds[k])
        if k >= 2:
            args += [owns[k - 2], to_even[max(k - 3, 0)], to_odd[k - 2]]
        args += [kvs[j] for j in (k - 1, k - 2) if j >= 0]
        args += rest
        if run is not None:
            args.append(run)
        outs = layer_call(k, args)
        out, kvs[k] = outs[0], outs[1]
        senders = senders_at(k)
        if senders:
            owns[k] = send(out, [(dev(s, c), dev(s + 1, c)) for s in senders for c in range(CTX)])
            to_odd[k] = send(out, [(dev(s, c), dev(s + 1, c + 1)) for s in senders for c in range(0, CTX, 2)])
            to_even[k] = send(out, [(dev(s, c), dev(s + 1, c - 1)) for s in senders for c in range(1, CTX, 2)])
        if k >= 2 * last:
            run, m = outs[2], k - 2 * last
            parts.append(run if m == last else send(run, [(dev(last, c), dev(m, c)) for c in range(CTX)]))
    kept = keep_call(parts)
    own = send(kept, [(dev(s, c), dev(c // 2, 2 * s + c % 2)) for s in range(STAGES) for c in range(CTX)])
    other = send(kept, [(dev(s, c), dev(c // 2, 2 * s + 1 - c % 2)) for s in range(STAGES) for c in range(CTX)])
    return merge_call(own, other)


def solution(mesh):
    return jax.shard_map(
        program,
        mesh=mesh,
        in_specs=(
            P(),
            P("ctx", None),
            P(),
            P("ctx", None),
            P("section", None),
            P("section", None, None),
            P("section", None, None),
            P("section", None),
            P("section", None, None),
            P("section", None, None),
            P(),
        ),
        out_specs=P("section", "ctx"),
        check_vma=False,
    )
```

```python
import functools
import math

import jax
import jax.numpy as jnp
from jax import lax
from jax.experimental import pallas as pl
from jax.experimental.pallas import tpu as pltpu
from jax.sharding import PartitionSpec as P

F32, BF = jnp.float32, jnp.bfloat16
R = 128
H = 8
D, FF = 1024, 2048
PAIRS = 8
STAGES, CTX, MICRO = 8, 16, 8
TICKS = MICRO + 2 * (STAGES - 1)
NEG = -1e30
AX = ("section", "ctx")


def dev(s, c):
    return s * CTX + c


def rms_scale(v):
    return lax.rsqrt(jnp.mean(v * v, axis=-1, keepdims=True) + 1e-05)


def shifted_column(row, before, shift):
    i = lax.broadcasted_iota(jnp.int32, (R, R), 0)
    j = lax.broadcasted_iota(jnp.int32, (R, R), 1)
    if not shift:
        return jnp.sum(jnp.where(i == j, row, 0.0), axis=1, keepdims=True)
    both = jnp.where(i == j + 1, row, 0.0) + jnp.where((i == 0) & (j == R - 1), before, 0.0)
    return jnp.sum(both, axis=1, keepdims=True)


def spin_row(spins, sample, block):
    start = pl.multiple_of(jnp.maximum(block, 0) * R, R)
    rows = spins[:, pl.ds(start, R)].astype(F32)
    return jnp.sum(jnp.where(lax.broadcasted_iota(jnp.int32, rows.shape, 0) == sample, rows, 0.0), axis=0, keepdims=True)


def load_kernel(*refs):
    sem = refs[-1]
    half = len(refs) // 2
    copies = [pltpu.make_async_copy(refs[i], refs[half + i], sem.at[i]) for i in range(half)]
    for copy in copies:
        copy.start()
    for copy in copies:
        copy.wait()


def load_call(values):
    return pl.pallas_call(
        load_kernel,
        out_shape=tuple(pltpu.VMEM(v.shape, v.dtype) for v in values),
        in_specs=[pl.BlockSpec(memory_space=pltpu.HBM)] * len(values),
        out_specs=(pl.BlockSpec(memory_space=pltpu.VMEM),) * len(values),
        scratch_shapes=[pltpu.SemaphoreType.DMA((len(values),))],
        compiler_params=pltpu.CompilerParams(vmem_limit_bytes=4 << 20),
        cost_estimate=pl.CostEstimate(flops=5 * 10**9, bytes_accessed=32 << 20, transcendentals=0),
        name="load",
    )(*(pltpu.with_memory_space_constraint(v, pltpu.HBM) for v in values))


def feed_kernel(mask, pos, behind, out):
    ctx = lax.axis_index("ctx")
    out[0:R, :] = pos[...]
    out[R + H:, :] = behind[...]
    columns = lax.broadcasted_iota(jnp.int32, (1, 128), 1)
    row = mask[...]
    flags = []
    for distance in (1, 2, 4):
        at = lax.broadcasted_iota(jnp.int32, (1, CTX), 1)
        hit = jnp.sum(jnp.where((at == ctx - distance) & (row == 1), 1.0, 0.0), axis=1, keepdims=True)
        flags.append(jnp.broadcast_to(hit, (H, 128)))
    flags.append(jnp.zeros((H, D - 384), F32))
    out[R:R + H, :] = jnp.concatenate(flags, axis=1).astype(BF)


def feed_call(mask, pos, behind):
    vm = pl.BlockSpec(memory_space=pltpu.VMEM)
    return pl.pallas_call(
        feed_kernel,
        out_shape=jax.ShapeDtypeStruct((2 * R + H, D), BF),
        in_specs=[vm] * 3,
        out_specs=vm,
        compiler_params=pltpu.CompilerParams(vmem_limit_bytes=4 << 20),
        name="feed",
    )(mask, pos, behind)


def layer_kernel(*refs, k):
    it = iter(refs)
    first = [next(it) for _ in range(2)] if k == 0 else None
    e_ref = next(it) if 0 < k < MICRO else None
    has_o = k >= 2
    o_ref, ca_ref, cb_ref = (next(it), next(it), next(it)) if has_o else (None, None, None)
    kv2 = next(it) if k >= 1 else None
    kv4 = next(it) if k >= 2 else None
    last_possible = k >= 2 * (STAGES - 1)
    wqkv, wout, wup, wdown, g1, g2, tok, whead, spins = [next(it) for _ in range(9)]
    msg_in = next(it) if k > 2 * (STAGES - 1) else None
    out_ref, kvo = next(it), next(it)
    msg = next(it) if last_possible else None
    x_s, h_s, kvc, q_s, att_s, hid_s, act_s = [next(it) for _ in range(7)]
    stage, ctx = lax.axis_index("section"), lax.axis_index("ctx")
    sample, odd = ctx // 2, ctx % 2
    m = k - 2 * stage
    b = 2 * m + odd

    if k < 2 * (STAGES - 1):
        @pl.when((m == -1) | (m == -2))
        def _():
            kvo[...] = jnp.zeros_like(kvo)

    @pl.when((m >= 0) & (m < MICRO))
    def _():
        if k < MICRO:
            @pl.when(stage == 0)
            def _():
                def embed(block, pos):
                    before = jnp.where(block > 0, spin_row(spins, sample, block - 1), 2.0)
                    t = shifted_column(spin_row(spins, sample, block), before, True)
                    rows = jnp.where(t == 0.0, tok[0:1, :], jnp.where(t == 1.0, tok[1:2, :], tok[2:3, :]))
                    return (rows + pos.astype(F32)).astype(BF)

                if k == 0:
                    x_s[0:R, :] = embed(b, first[0][...])
                    x_s[R:, :] = embed(b - 1, first[1][...])
                    lanes = lax.broadcasted_iota(jnp.int32, (H, D), 1)
                    h_s[...] = jnp.where((lanes < 128) & (odd == 1), 1.0, 0.0).astype(BF)
                else:
                    x_s[0:R, :] = embed(b, e_ref[0:R, :])
                    x_s[R:, :] = embed(b - 1, e_ref[R + H:2 * R + H, :])
                    h_s[...] = e_ref[R:R + H, :]
        if has_o:
            @pl.when(stage > 0)
            def _():
                x_s[0:R, :] = o_ref[0:R, :]
                h_s[...] = o_ref[R:R + H, :]

                @pl.when(odd == 0)
                def _():
                    x_s[R:, :] = ca_ref[0:R, :]

                @pl.when(odd == 1)
                def _():
                    x_s[R:, :] = cb_ref[0:R, :]

        xf = x_s[...].astype(F32)
        a = (xf * rms_scale(xf) * g1[...]).astype(BF)
        q_s[...] = (jnp.dot(a[0:R, :], wqkv[:, :D], preferred_element_type=F32) * 0.125).astype(BF)
        for j in range(2):
            p = jnp.dot(a, wqkv[:, (j + 1) * D:(j + 2) * D], preferred_element_type=F32).astype(BF)
            kvo[:, j * D:(j + 1) * D] = p[:R]
            kvc[:, j * D:(j + 1) * D] = p[R:]

        lane = lax.broadcasted_iota(jnp.int32, (R, 128), 1)
        row = lax.broadcasted_iota(jnp.int32, (R, 128), 0)
        causal = jnp.where(lane <= row, 0.0, NEG)
        causal2 = jnp.concatenate([causal, causal], axis=0)
        flags = h_s[0:1, 0:384].astype(F32)
        f1, f2, f4 = [jnp.where(flags[:, i * 128:(i + 1) * 128] > 0.5, 0.0, NEG) for i in range(3)]
        ones = jnp.ones((2 * R, 128), BF)
        low = lane < 64
        nt = (((1,), (1,)), ((), ()))
        for h in range(PAIRS):
            o, v = slice(h * 128, h * 128 + 128), slice(D + h * 128, D + h * 128 + 128)
            q = q_s[:, o]
            zero = jnp.zeros_like(q)
            q2 = jnp.concatenate([jnp.where(low, q, zero), jnp.where(low, zero, q)], axis=0)
            ka = jnp.concatenate([kvo[:, o], kvc[:, o]], axis=0)
            blank = jnp.zeros((R, 128), BF)
            kb = jnp.concatenate([kv2[:, o] if kv2 is not None else blank, kv4[:, o] if kv4 is not None else blank], axis=0)
            sa = lax.dot_general(q2, ka, nt, preferred_element_type=F32)
            sb = lax.dot_general(q2, kb, nt, preferred_element_type=F32)
            s0 = sa[:, :128] + causal2
            s1 = sa[:, 128:] + f1
            s2 = sb[:, :128] + f2
            s4 = sb[:, 128:] + f4
            top = jnp.max(jnp.maximum(jnp.maximum(s0, s1), jnp.maximum(s2, s4)), axis=-1, keepdims=True)
            pa = jnp.concatenate([jnp.exp(s0 - top).astype(BF), jnp.exp(s1 - top).astype(BF)], axis=1)
            pb = jnp.concatenate([jnp.exp(s2 - top).astype(BF), jnp.exp(s4 - top).astype(BF)], axis=1)
            va = jnp.concatenate([jnp.concatenate([kvo[:, v], kvc[:, v]], axis=0), ones], axis=1)
            vb = jnp.concatenate([jnp.concatenate([kv2[:, v] if kv2 is not None else blank, kv4[:, v] if kv4 is not None else blank], axis=0), ones], axis=1)
            r = jnp.dot(pa, va, preferred_element_type=F32) + jnp.dot(pb, vb, preferred_element_type=F32)
            num = jnp.where(low, r[:R, :128], r[R:, :128])
            den = jnp.where(low, r[:R, 128:], r[R:, 128:])
            att_s[:, o] = (num / den).astype(BF)

        hid_s[...] = x_s[0:R, :].astype(F32) + jnp.dot(att_s[...], wout[...], preferred_element_type=F32)
        hid = hid_s[...]
        lifted = (hid * rms_scale(hid) * g2[...]).astype(BF)
        for j in range(2):
            up = jnp.dot(lifted, wup[:, j * D:(j + 1) * D], preferred_element_type=F32)
            act_s[:, j * D:(j + 1) * D] = jax.nn.gelu(up).astype(BF)
        out = (hid_s[...] + jnp.dot(act_s[...], wdown[...], preferred_element_type=F32)).astype(BF)
        out_ref[0:R, :] = out
        out_ref[R:, :] = h_s[...]
        if last_possible:
            @pl.when(stage == STAGES - 1)
            def _():
                y = out_ref[0:R, :].astype(F32)
                logits = jnp.sum(y * rms_scale(y) * whead[...], axis=-1, keepdims=True)
                spin = shifted_column(spin_row(spins, sample, b), None, False)
                terms = math.log(2.0) - jax.nn.softplus((1.0 - 2.0 * spin) * logits)
                i = lax.broadcasted_iota(jnp.int32, (R, R), 0)
                j = lax.broadcasted_iota(jnp.int32, (R, R), 1)
                cum = jnp.sum(jnp.where(i <= j, terms, 0.0), axis=0, keepdims=True)
                tot = jnp.sum(jnp.broadcast_to(terms, (R, R)), axis=0, keepdims=True)
                run = jnp.zeros((1, 128), F32) if msg_in is None else msg_in[1:2, :]
                msg[...] = jnp.concatenate([cum + run, tot + run, run, jnp.zeros((5, 128), F32)], axis=0)


def keep_kernel(*refs):
    stage = lax.axis_index("section")
    for m in range(MICRO):
        @pl.when(stage == m)
        def _():
            refs[-1][...] = refs[m][...]


def keep_call(parts):
    vm = pl.BlockSpec(memory_space=pltpu.VMEM)
    return pl.pallas_call(
        keep_kernel,
        out_shape=jax.ShapeDtypeStruct((8, 128), F32),
        in_specs=[vm] * MICRO,
        out_specs=vm,
        compiler_params=pltpu.CompilerParams(vmem_limit_bytes=4 << 20),
        name="keep",
    )(*parts)


def merge_kernel(own, other, out):
    odd = lax.axis_index("ctx") % 2
    out[...] = 0.5 * (own[0:1, :] + jnp.where(odd == 1, other[1:2, :], other[2:3, :]))


def merge_call(own, other):
    vm = pl.BlockSpec(memory_space=pltpu.VMEM)
    return pl.pallas_call(
        merge_kernel,
        out_shape=jax.ShapeDtypeStruct((1, 128), F32),
        in_specs=[vm, vm],
        out_specs=vm,
        compiler_params=pltpu.CompilerParams(vmem_limit_bytes=4 << 20),
        name="merge",
    )(own, other)


def layer_call(k, args):
    vm = pl.BlockSpec(memory_space=pltpu.VMEM)
    shapes = [jax.ShapeDtypeStruct((R + H, D), BF), jax.ShapeDtypeStruct((R, 2 * D), BF)]
    if k >= 2 * (STAGES - 1):
        shapes.append(jax.ShapeDtypeStruct((8, 128), F32))
    return pl.pallas_call(
        functools.partial(layer_kernel, k=k),
        out_shape=tuple(shapes),
        in_specs=[vm] * len(args),
        out_specs=(vm,) * len(shapes),
        scratch_shapes=[
            pltpu.VMEM((2 * R, D), BF),
            pltpu.VMEM((H, D), BF),
            pltpu.VMEM((R, 2 * D), BF),
            pltpu.VMEM((R, D), BF),
            pltpu.VMEM((R, D), BF),
            pltpu.VMEM((R, D), F32),
            pltpu.VMEM((R, FF), BF),
        ],
        compiler_params=pltpu.CompilerParams(vmem_limit_bytes=20 << 20),
        cost_estimate=pl.CostEstimate(flops=4 * 10**9, bytes_accessed=10**6, transcendentals=10**6),
    )(*args)


def senders_at(k):
    return (0, 1, 2, 3) if k < 8 else (1, 2, 3, 4, 5, 6) if k < 20 else ()


def program(spins, block_mask, tok_embed, pos_embed, norm1_gain, w_qkv, w_out, norm2_gain, w_up, w_down, w_head):
    def send(value, pairs):
        return lax.ppermute(value, AX, pairs)

    first_own = send(pos_embed, [(dev(s, p), dev(0, 2 * s + p)) for s in range(STAGES) for p in range(2)])
    first_copy = send(pos_embed, [(dev(s, 0), dev(0, 2 * s + 1)) for s in range(STAGES)])
    behind = send(pos_embed, [(dev(s, c), dev(s, c + 1)) for s in range(STAGES) for c in range(CTX - 1)])
    loaded = load_call(
        (w_qkv[0], w_out[0], w_up[0], w_down[0], norm1_gain, norm2_gain, tok_embed, w_head[None], spins, pos_embed, block_mask)
    )
    rest, (pos, mask) = loaded[:9], loaded[9:]
    double = feed_call(mask, pos, behind)

    def feed(m):
        return send(double, [(dev(s, 2 * m + p), dev(0, 2 * s + p)) for s in range(STAGES) for p in range(2)])

    feeds = {m: feed(m) for m in range(1, 4)}
    kvs, owns, to_odd, to_even = {}, {}, {}, {}
    last = STAGES - 1
    run, parts = None, []
    for k in range(TICKS):
        args = []
        if k == 0:
            args += [first_own, first_copy]
        elif k < MICRO:
            args.append(feeds[k])
        if k >= 2:
            args += [owns[k - 2], to_even[max(k - 3, 0)], to_odd[k - 2]]
        args += [kvs[j] for j in (k - 1, k - 2) if j >= 0]
        args += rest
        if run is not None:
            args.append(run)
        outs = layer_call(k, args)
        out, kvs[k] = outs[0], outs[1]
        senders = senders_at(k)
        if senders:
            owns[k] = send(out, [(dev(s, c), dev(s + 1, c)) for s in senders for c in range(CTX)])
            to_odd[k] = send(out, [(dev(s, c), dev(s + 1, c + 1)) for s in senders for c in range(0, CTX, 2)])
            to_even[k] = send(out, [(dev(s, c), dev(s + 1, c - 1)) for s in senders for c in range(1, CTX, 2)])
        if k == 0:
            double, _ = lax.optimization_barrier((double, out))
            for m in range(4, MICRO):
                feeds[m] = feed(m)
        if k >= 2 * last:
            run = outs[2]
            parts.append(run)
    parts = list(lax.optimization_barrier(tuple(parts)))
    for m in range(last):
        parts[m] = send(parts[m], [(dev(last, c), dev(m, c)) for c in range(CTX)])
    kept = keep_call(parts)
    own = send(kept, [(dev(s, c), dev(c // 2, 2 * s + c % 2)) for s in range(STAGES) for c in range(CTX)])
    other = send(kept, [(dev(s, c), dev(c // 2, 2 * s + 1 - c % 2)) for s in range(STAGES) for c in range(CTX)])
    return merge_call(own, other)


def solution(mesh):
    return jax.shard_map(
        program,
        mesh=mesh,
        in_specs=(
            P(),
            P("ctx", None),
            P(),
            P("ctx", None),
            P("section", None),
            P("section", None, None),
            P("section", None, None),
            P("section", None),
            P("section", None, None),
            P("section", None, None),
            P(),
        ),
        out_specs=P("section", "ctx"),
        check_vma=False,
    )
```
